32 devices in a mesh: row: 8 (over z, core), col: 4 (over y, x).
Axes of the slice: x: 2, y: 2, z: 4, core: 2. Of those that a mesh axis runs over, the one named last changes fastest.
Arguments:
- matrix: float32 [12288, 12288], P('row', 'col'), may hold values from -8 to 8
Outputs:
- updated: float32 [12288, 12288], P('row', 'col')
- reflectors: float32 [16, 12288], replicated
- coefficients: float32 [2, 16], replicated
The draws below stay inside these ranges and needn't reach their ends.
All inputs are finite; a program needn't handle non-finite values.
Results may differ from the reference program's by a relative error of at most 0.0003.
Values sent between devices are 32-bit elements; how exact they have to be, the bound alone decides.
A program may use at most 64 MiB of HBM per device.

```python
import jax
import jax.numpy as jnp
from jax import lax

ORDER = 12288
PANEL_COLUMNS = 16


def draw_matrix(key, part):
    first = jax.random.fold_in(jax.random.fold_in(key, 11), 0)
    raw = jax.random.normal(first, (ORDER, ORDER), jnp.float32)
    sym = (raw + raw.T) * jnp.float32(0.7071067811865476)
    return jnp.clip(sym, -8.0, 8.0)


def setup_inputs(seed: int = 0) -> dict:
    splits = jax.random.split(jax.random.key(seed), 2)
    return {
        "matrix": draw_matrix(jax.random.fold_in(splits[1], 71), 0),
    }


HIGH = lax.Precision.HIGHEST

def reference(matrix):
    order = matrix.shape[0]
    positions = jnp.arange(order, dtype=jnp.int32)
    reflectors = jnp.zeros((PANEL_COLUMNS, order), jnp.float32)
    reflected_images = jnp.zeros((PANEL_COLUMNS, order), jnp.float32)
    reflector_scales = []
    below_diagonal = []
    for step in range(PANEL_COLUMNS):
        column = matrix[:, step] - jnp.dot(reflected_images[:, step], reflectors, precision=HIGH) - jnp.dot(reflectors[:, step], reflected_images, precision=HIGH)
        below = jnp.where(positions > step, column, 0.0)
        leading = column[step + 1]
        norm_value = jnp.sqrt(jnp.sum(below * below))
        reflector = jnp.where(positions == step + 1, 1.0, below / (leading + norm_value))
        reflector_scale = 1.0 + leading / norm_value
        product = jnp.dot(matrix, reflector, precision=HIGH)
        images_dot = jnp.dot(reflected_images, reflector, precision=HIGH)
        reflect_dot = jnp.dot(reflectors, reflector, precision=HIGH)
        image = reflector_scale * (product - jnp.dot(images_dot, reflectors, precision=HIGH) - jnp.dot(reflect_dot, reflected_images, precision=HIGH))
        image = image - 0.5 * reflector_scale * jnp.sum(image * reflector) * reflector
        reflectors = reflectors.at[step].set(reflector)
        reflected_images = reflected_images.at[step].set(image)
        reflector_scales.append(reflector_scale)
        below_diagonal.append(-norm_value)
    left_side = jnp.concatenate([reflectors, reflected_images], axis=0)
    right_side = jnp.concatenate([reflected_images, reflectors], axis=0)
    updated = matrix - jnp.einsum('kr,kc->rc', left_side, right_side, precision=HIGH)
    coefficients = jnp.stack([jnp.stack(reflector_scales), jnp.stack(below_diagonal)])
    return (updated, reflectors, coefficients)
```

```python
import jax
import jax.numpy as jnp
from jax import lax
from jax.experimental import pallas as pl
from jax.experimental.pallas import tpu as pltpu
from jax.sharding import PartitionSpec as P

K = 16
HEAD = 24
LANES = 128
MESH = pl.DeviceIdType.MESH


def lane_pick(block, lanes, index):
    return jnp.sum(jnp.where(lanes == index, block, 0.0), axis=1, keepdims=True)


def panel_kernel(rows, cols, n_row, n_col, mat, v_out, wc_out, vw_out, coef_out, kap_out,
                 tile, panel, vw, msg, recv, gout, c0_ref, u_ref, p_ref, au_ref, b0_ref,
                 vu_ref, wu_ref, s_ref, kmsg, krecv,
                 load_sem, panel_sem, psend_sem, send_sem, recv_sem, gsend_sem, v_sem, w_sem,
                 ksend_sem, k_sem):
    width = rows + LANES
    halves = cols // rows
    r = lax.axis_index("row")
    c = lax.axis_index("col")
    blocks = rows // LANES
    ctiles = cols // LANES

    def chunk(i):
        part = pl.ds(pl.multiple_of(i * LANES, LANES), LANES)
        return pltpu.make_async_copy(mat.at[part], tile.at[part], load_sem.at[i])

    def start_chunk(i, carry):
        chunk(i).start()
        return carry

    barrier = pltpu.get_barrier_semaphore()
    for dr in range(n_row):
        for dc in range(n_col):
            if dr or dc:
                pl.semaphore_signal(barrier, inc=1, device_id=(lax.rem(r + dr, n_row), lax.rem(c + dc, n_col)),
                                    device_id_type=MESH)
    vw[...] = jnp.zeros_like(vw)
    u_ref[...] = jnp.zeros_like(u_ref)
    p_ref[...] = jnp.zeros_like(p_ref)
    au_ref[...] = jnp.zeros_like(au_ref)
    vu_ref[...] = jnp.zeros_like(vu_ref)
    wu_ref[...] = jnp.zeros_like(wu_ref)
    s_ref[...] = jnp.zeros_like(s_ref)
    coef_out[...] = jnp.zeros_like(coef_out)
    pl.semaphore_wait(barrier, n_row * n_col - 1)

    def panel_copy(h, dc, local):
        src = mat.at[0:HEAD, h * rows:(h + 1) * rows]
        dst = panel.at[:, 0:rows]
        if local:
            return pltpu.make_async_copy(src, dst, panel_sem)
        return pltpu.make_async_remote_copy(
            src, dst, psend_sem, panel_sem,
            device_id=(halves * c + h, lax.rem(c + dc, n_col)), device_id_type=MESH)

    def head_copy(dr, dc, local):
        src = mat.at[0:HEAD, 0:LANES]
        dst = panel.at[:, rows:width]
        if local:
            return pltpu.make_async_copy(src, dst, panel_sem)
        return pltpu.make_async_remote_copy(src, dst, psend_sem, panel_sem, device_id=(dr, dc), device_id_type=MESH)

    def each_target(fn_remote, fn_local):
        for dc in range(n_col):
            for h in range(halves):
                if dc:
                    fn_remote(h, dc)
                else:
                    own = halves * c + h == r
                    pl.when(jnp.logical_not(own))(lambda h=h, dc=dc: fn_remote(h, dc))
                    if fn_local is not None:
                        pl.when(own)(lambda h=h, dc=dc: fn_local(h, dc))

    @pl.when(r == 0)
    def _():
        @pl.when(c == 0)
        def _():
            for dr in range(n_row):
                for dc in range(n_col):
                    head_copy(dr, dc, dr == 0 and dc == 0).start()
        each_target(lambda h, dc: panel_copy(h, dc, False).start(), lambda h, dc: panel_copy(h, dc, True).start())

    lax.fori_loop(0, blocks, start_chunk, 0)
    pltpu.make_async_copy(panel, panel, panel_sem).wait()

    @pl.when(r == 0)
    def _():
        @pl.when(c == 0)
        def _():
            for dr in range(n_row):
                for dc in range(n_col):
                    if dr or dc:
                        head_copy(dr, dc, False).wait_send()
        each_target(lambda h, dc: panel_copy(h, dc, False).wait_send(), None)

    c0_ref[...] = panel[0:1, :]
    lane = lax.broadcasted_iota(jnp.int32, (1, width), 1)
    pos = jnp.where(lane < rows, lane + r * rows, jnp.where(lane < rows + HEAD, lane - rows, -1))
    l128 = lax.broadcasted_iota(jnp.int32, (1, LANES), 1)
    k16 = lax.broadcasted_iota(jnp.int32, (K, 1), 0)

    def send_copy(j, h, dc, local):
        src = msg.at[j, h]
        dst = recv.at[j, r]
        if local:
            return pltpu.make_async_copy(src, dst, recv_sem.at[j])
        return pltpu.make_async_remote_copy(
            src, dst, send_sem, recv_sem.at[j],
            device_id=(halves * c + h, lax.rem(c + dc, n_col)), device_id_type=MESH)

    def v_copy(j, dr):
        return pltpu.make_async_remote_copy(
            gout.at[j, 0], v_out.at[j, r], gsend_sem, v_sem,
            device_id=(lax.rem(r + dr, n_row), c), device_id_type=MESH)

    def w_copy(j, dr):
        return pltpu.make_async_remote_copy(
            gout.at[j, 1], wc_out.at[j, lax.rem(r, halves)], gsend_sem, w_sem,
            device_id=(lax.rem(r + dr, n_row), c), device_id_type=MESH)

    def k_copy(dr):
        return pltpu.make_async_remote_copy(
            kmsg, krecv.at[r], ksend_sem, k_sem,
            device_id=(lax.rem(r + dr, n_row), c), device_id_type=MESH)

    gives_w = r // halves == c

    def spread(i):
        row = b0_ref[:, pl.ds(pl.multiple_of(i * LANES, LANES), LANES)]
        return jnp.broadcast_to(row, (LANES, LANES)).T

    def step(j, carry):
        m2 = pos > j + 1
        c0 = c0_ref[...]
        b0 = jnp.where(m2, c0, 0.0)
        b0_ref[...] = b0
        u_prev = u_ref[...]
        p_prev = p_ref[...]

        b_loc = b0[:, :rows]
        dvw = jnp.sum(vw[:, :rows] * b_loc, axis=1, keepdims=True)
        dpn = jnp.sum(panel[:, :rows] * b_loc, axis=1, keepdims=True)
        n0 = jnp.sum(b_loc * b_loc, axis=1, keepdims=True)
        kp = jnp.sum(u_prev[:, :rows] * p_prev[:, :rows], axis=1, keepdims=True)
        s32 = lax.broadcasted_iota(jnp.int32, (2 * K, LANES), 0)
        t32 = lax.broadcasted_iota(jnp.int32, (2 * K, LANES), 1)
        s24 = lax.broadcasted_iota(jnp.int32, (HEAD, LANES), 0)
        t24 = lax.broadcasted_iota(jnp.int32, (HEAD, LANES), 1)
        sc = jnp.sum(jnp.where(s32 == t32, dvw, 0.0), axis=0, keepdims=True)
        sc += jnp.sum(jnp.where(s24 + 2 * K == t24, dpn, 0.0), axis=0, keepdims=True)
        sc += jnp.where(l128 == 2 * K + HEAD, n0, 0.0) + jnp.where(l128 == 2 * K + HEAD + 1, kp, 0.0)

        def block(i, state):
            bc, accs = state
            pl.when(j == 0)(lambda: chunk(i).wait())
            nxt = spread(jnp.minimum(i + 1, blocks - 1))
            b3 = bc.reshape(LANES // 8, 8, LANES)
            part = pl.ds(pl.multiple_of(i * LANES, LANES), LANES)
            new = []
            for t in range(ctiles):
                x = tile[part, t * LANES:(t + 1) * LANES].reshape(LANES // 8, 8, LANES)
                new.append(accs[t] + jnp.sum(x * b3, axis=0))
            return nxt, tuple(new)

        zero = jnp.zeros((8, LANES), jnp.float32)
        _, accs = lax.fori_loop(0, blocks, block, (spread(0), (zero,) * ctiles))
        per = rows // LANES
        for h in range(halves):
            for t in range(per):
                msg[j, h, :, t * LANES:(t + 1) * LANES] = jnp.sum(accs[h * per + t], axis=0, keepdims=True)
            msg[j, h, :, rows:width] = sc

        each_target(lambda h, dc: send_copy(j, h, dc, False).start(), lambda h, dc: send_copy(j, h, dc, True).start())
        pltpu.make_async_copy(recv.at[j], recv.at[j], recv_sem.at[j]).wait()

        tot = jnp.sum(recv[j], axis=0)
        sc = tot[:, rows:width]
        wide = jnp.broadcast_to(sc, (2 * K, LANES))
        dots = jnp.sum(jnp.where(s32 == t32, wide, 0.0), axis=1, keepdims=True)
        n0 = sc[:, 2 * K + HEAD:2 * K + HEAD + 1]
        kp = sc[:, 2 * K + HEAD + 1:2 * K + HEAD + 2]
        tau_prev = s_ref[0:1, 0:1]
        bb_prev = s_ref[1:2, 0:1]
        kap = 0.5 * tau_prev * kp
        kap_out[pl.ds(j, 1), :] = jnp.broadcast_to(kap, (1, LANES))
        vw[pl.ds(K + j - 1, 1), :] = p_prev - kap * u_prev
        pj = panel[pl.ds(j, 1), :]
        pj1 = panel[pl.ds(j + 1, 1), :]
        col = c0 + 2.0 * kap * u_prev
        uj1 = lane_pick(u_prev[:, rows:width], l128, j + 1)
        aq = au_ref[...] - pj - uj1 * pj1
        yhead = jnp.where(l128 < HEAD, pltpu.roll(sc, LANES - 2 * K, 1), 0.0)
        y = jnp.concatenate([tot[:, :rows], yhead], axis=1) + 2.0 * kap * aq
        vb = dots[:K]
        wb = dots[K:]
        last = k16 == j - 1
        n1 = jnp.sum(jnp.where(last, vb, 0.0), axis=0, keepdims=True)
        b2 = jnp.maximum(n0 + 4.0 * kap * (n1 + kap * (bb_prev - uj1 * uj1)), 0.0)
        lead = lane_pick(col[:, rows:width], l128, j + 1)
        sig = jnp.sqrt(b2 + lead * lead)
        inv = 1.0 / (lead + sig)
        tau = 1.0 + lead / sig
        u = jnp.where(m2, col * inv, 0.0) + jnp.where(pos == j + 1, 1.0, 0.0)
        au = y * inv + pj1

        head = vw[:, rows:width]
        hj = lane_pick(head, l128, j)
        hj1 = lane_pick(head, l128, j + 1)
        uu = bb_prev + 1.0
        vup = jnp.where(last, uu, vu_ref[:, 0:1])
        wup = jnp.where(last, kp - kap * uu, wu_ref[:, 0:1])
        wb = jnp.where(last, wb - kap * vb, wb)
        vu = (vb + 2.0 * kap * (vup - hj[:K] - uj1 * hj1[:K])) * inv + hj1[:K]
        wu = (wb + 2.0 * kap * (wup - hj[K:] - uj1 * hj1[K:])) * inv + hj1[K:]
        v_all = vw[0:K, :]
        w_all = vw[K:2 * K, :]
        p = tau * (au - jnp.sum(v_all * wu + w_all * vu, axis=0, keepdims=True))
        pj1_entry = lane_pick(p[:, rows:width], l128, j + 1)
        c0n = pj1 - jnp.sum(v_all * hj1[K:] + w_all * hj1[:K], axis=0, keepdims=True) - pj1_entry * u - p
        gout[j, 0] = u[:, :rows]
        gout[j, 1] = p[:, :rows]
        c0_ref[...] = c0n
        u_ref[...] = u
        p_ref[...] = p
        au_ref[...] = au
        vu_ref[...] = jnp.broadcast_to(vu, (K, LANES))
        wu_ref[...] = jnp.broadcast_to(wu, (K, LANES))
        s_ref[0:1, :] = jnp.broadcast_to(tau, (1, LANES))
        s_ref[1:2, :] = jnp.broadcast_to(b2 * inv * inv, (1, LANES))
        coef_out[0:1, :] = jnp.where(l128 == j, tau, coef_out[0:1, :])
        coef_out[1:2, :] = jnp.where(l128 == j, -sig, coef_out[1:2, :])
        vw[pl.ds(j, 1), :] = u
        vw[pl.ds(K + j, 1), :] = p

        for dr in range(1, n_row):
            v_copy(j, dr).start()
        pltpu.make_async_copy(gout.at[j, 0], v_out.at[j, r], v_sem).start()

        @pl.when(gives_w)
        def _():
            for dr in range(1, n_row):
                w_copy(j, dr).start()
            pltpu.make_async_copy(gout.at[j, 1], wc_out.at[j, lax.rem(r, halves)], w_sem).start()
        return carry

    lax.fori_loop(0, K, step, 0)

    u = u_ref[...]
    p = p_ref[...]
    kp = jnp.sum(u[:, :rows] * p[:, :rows], axis=1, keepdims=True)
    kmsg[...] = jnp.broadcast_to(kp, (1, LANES))
    for dr in range(1, n_row):
        k_copy(dr).start()
    pltpu.make_async_copy(kmsg, krecv.at[r], k_sem).start()
    pltpu.make_async_copy(krecv, krecv, k_sem).wait()
    kap = 0.5 * s_ref[0:1, :] * jnp.sum(krecv[...], axis=0)
    kap_out[K:K + 1, :] = kap
    vw[2 * K - 1:2 * K, :] = p - kap[:, 0:1] * u
    vw_out[...] = vw[:, :rows]

    def drain(j, carry):
        each_target(lambda h, dc: send_copy(j, h, dc, False).wait_send(), None)
        for dr in range(1, n_row):
            v_copy(j, dr).wait_send()

        @pl.when(gives_w)
        def _():
            for dr in range(1, n_row):
                w_copy(j, dr).wait_send()
        return carry

    lax.fori_loop(0, K, drain, 0)
    for dr in range(1, n_row):
        k_copy(dr).wait_send()
    pltpu.make_async_copy(v_out, v_out, v_sem).wait()
    pltpu.make_async_copy(wc_out, wc_out, w_sem).wait()


def pieces(x):
    hi = lax.reduce_precision(x, 8, 7)
    rest = x - hi
    mid = lax.reduce_precision(rest, 8, 7)
    low = lax.reduce_precision(rest - mid, 8, 7)
    return [part.astype(jnp.bfloat16) for part in (hi, mid, low)]


def make_per_device(n_row, n_col):
    def per_device(matrix):
        rows, cols = matrix.shape
        halves = cols // rows
        width = rows + LANES
        f32 = jnp.float32
        vmem = pl.BlockSpec(memory_space=pltpu.VMEM)
        anyspace = pl.BlockSpec(memory_space=pl.ANY)
        dma = pltpu.SemaphoreType.DMA

        def kernel(*refs):
            panel_kernel(rows, cols, n_row, n_col, *refs)

        v_full, wc, vw, coef, kap = pl.pallas_call(
            kernel,
            out_shape=(
                jax.ShapeDtypeStruct((K, n_row, 1, rows), f32),
                jax.ShapeDtypeStruct((K, halves, 1, rows), f32),
                jax.ShapeDtypeStruct((2 * K, rows), f32),
                jax.ShapeDtypeStruct((2, LANES), f32),
                jax.ShapeDtypeStruct((K + 1, LANES), f32),
            ),
            in_specs=[anyspace],
            out_specs=(anyspace, anyspace, vmem, vmem, vmem),
            scratch_shapes=[
                pltpu.VMEM((rows, cols), f32),
                pltpu.VMEM((HEAD, width), f32),
                pltpu.VMEM((2 * K, width), f32),
                pltpu.VMEM((K, halves, 1, width), f32),
                pltpu.VMEM((K, n_row, 1, width), f32),
                pltpu.VMEM((K, 2, 1, rows), f32),
                pltpu.VMEM((1, width), f32),
                pltpu.VMEM((1, width), f32),
                pltpu.VMEM((1, width), f32),
                pltpu.VMEM((1, width), f32),
                pltpu.VMEM((1, width), f32),
                pltpu.VMEM((K, LANES), f32),
                pltpu.VMEM((K, LANES), f32),
                pltpu.VMEM((8, LANES), f32),
                pltpu.VMEM((1, LANES), f32),
                pltpu.VMEM((n_row, 1, LANES), f32),
                dma((rows // LANES,)),
                dma, dma, dma,
                dma((K,)),
                dma, dma, dma, dma, dma,
            ],
            compiler_params=pltpu.CompilerParams(
                collective_id=0, has_side_effects=True, vmem_limit_bytes=48 * 1024 * 1024),
        )(matrix)
        reflectors = v_full.reshape(K, n_row * rows)
        c = lax.axis_index("col")
        v_cols = lax.dynamic_slice_in_dim(reflectors, c * cols, cols, 1)
        w_cols = wc.reshape(K, cols) - kap[1:, 0:1] * v_cols
        left = pieces(vw)
        right = pieces(jnp.concatenate([w_cols, v_cols], axis=0))
        order = ((0, 0), (0, 1), (1, 0), (1, 1), (0, 2), (2, 0))
        big_left = jnp.concatenate([left[a] for a, _ in order], axis=0)
        big_right = jnp.concatenate([right[b] for _, b in order], axis=0)
        change = lax.dot_general(big_left, big_right, (((0,), (0,)), ((), ())), preferred_element_type=f32)
        return matrix - change, reflectors, coef[:, :K]
    return per_device


def solution(mesh):
    return jax.shard_map(
        make_per_device(mesh.shape["row"], mesh.shape["col"]),
        mesh=mesh,
        in_specs=(P("row", "col"),),
        out_specs=(P("row", "col"), P(), P()),
        check_vma=False,
    )
```

```python
import jax
import jax.numpy as jnp
from jax import lax
from jax.experimental import pallas as pl
from jax.experimental.pallas import tpu as pltpu
from jax.sharding import PartitionSpec as P

K = 16
HEAD = 24
LANES = 128
MESH = pl.DeviceIdType.MESH


def lane_pick(block, lanes, index):
    return jnp.sum(jnp.where(lanes == index, block, 0.0), axis=1, keepdims=True)


def panel_kernel(rows, cols, n_row, n_col, mat, v_out, wc_out, vw_out, coef_out, kap_out,
                 tile, first, panel, vw, msg, recv, gout, c0_ref, u_ref, p_ref, au_ref, b0_ref,
                 vu_ref, wu_ref, s_ref, kmsg, krecv,
                 load_sem, first_sem, panel_sem, head_sem, psend_sem, send_sem, recv_sem, gsend_sem, v_sem, w_sem,
                 ksend_sem, k_sem):
    width = rows + LANES
    halves = cols // rows
    r = lax.axis_index("row")
    c = lax.axis_index("col")
    blocks = rows // LANES
    ctiles = cols // LANES

    def chunk(i):
        part = pl.ds(pl.multiple_of(i * LANES, LANES), LANES)
        return pltpu.make_async_copy(mat.at[part], tile.at[part], load_sem.at[i])

    def start_chunk(i, carry):
        chunk(i).start()
        return carry

    first_copy = pltpu.make_async_copy(mat.at[:, 0:LANES], first, first_sem)
    pl.when(c == 0)(lambda: first_copy.start())
    lax.fori_loop(0, blocks, start_chunk, 0)

    barrier = pltpu.get_barrier_semaphore()
    for dr in range(n_row):
        for dc in range(n_col):
            if dr or dc:
                pl.semaphore_signal(barrier, inc=1, device_id=(lax.rem(r + dr, n_row), lax.rem(c + dc, n_col)),
                                    device_id_type=MESH)

    @pl.when(c == 0)
    def _():
        first_copy.wait()
        for i in range(blocks):
            part = slice(i * LANES, (i + 1) * LANES)
            panel[:, part] = first[part, :].T[0:HEAD, :]

    vw[...] = jnp.zeros_like(vw)
    u_ref[...] = jnp.zeros_like(u_ref)
    p_ref[...] = jnp.zeros_like(p_ref)
    au_ref[...] = jnp.zeros_like(au_ref)
    vu_ref[...] = jnp.zeros_like(vu_ref)
    wu_ref[...] = jnp.zeros_like(wu_ref)
    s_ref[...] = jnp.zeros_like(s_ref)
    coef_out[...] = jnp.zeros_like(coef_out)
    pl.semaphore_wait(barrier, n_row * n_col - 1)

    def panel_copy(dc):
        return pltpu.make_async_remote_copy(
            panel.at[:, 0:rows], panel.at[:, 0:rows], psend_sem, panel_sem,
            device_id=(r, dc), device_id_type=MESH)

    def head_copy(dr, dc):
        src = mat.at[0:HEAD, 0:LANES]
        dst = panel.at[:, rows:width]
        if dr == 0 and dc == 0:
            return pltpu.make_async_copy(src, dst, head_sem)
        return pltpu.make_async_remote_copy(src, dst, psend_sem, head_sem, device_id=(dr, dc), device_id_type=MESH)

    def each_target(fn_remote, fn_local):
        for dc in range(n_col):
            for h in range(halves):
                if dc:
                    fn_remote(h, dc)
                else:
                    own = halves * c + h == r
                    pl.when(jnp.logical_not(own))(lambda h=h, dc=dc: fn_remote(h, dc))
                    if fn_local is not None:
                        pl.when(own)(lambda h=h, dc=dc: fn_local(h, dc))

    @pl.when(c == 0)
    def _():
        @pl.when(r == 0)
        def _():
            for dr in reversed(range(n_row)):
                for dc in reversed(range(n_col)):
                    head_copy(dr, dc).start()
        for dc in reversed(range(1, n_col)):
            panel_copy(dc).start()

    pltpu.make_async_copy(panel.at[:, rows:width], panel.at[:, rows:width], head_sem).wait()

    @pl.when(c != 0)
    def _():
        pltpu.make_async_copy(panel.at[:, 0:rows], panel.at[:, 0:rows], panel_sem).wait()

    c0_ref[...] = panel[0:1, :]
    lane = lax.broadcasted_iota(jnp.int32, (1, width), 1)
    pos = jnp.where(lane < rows, lane + r * rows, jnp.where(lane < rows + HEAD, lane - rows, -1))
    l128 = lax.broadcasted_iota(jnp.int32, (1, LANES), 1)
    k16 = lax.broadcasted_iota(jnp.int32, (K, 1), 0)

    def send_copy(j, h, dc, local):
        src = msg.at[j, h]
        dst = recv.at[j, r]
        if local:
            return pltpu.make_async_copy(src, dst, recv_sem.at[j])
        return pltpu.make_async_remote_copy(
            src, dst, send_sem, recv_sem.at[j],
            device_id=(halves * c + h, lax.rem(c + dc, n_col)), device_id_type=MESH)

    def v_copy(j, dr):
        return pltpu.make_async_remote_copy(
            gout.at[j, 0], v_out.at[j, r], gsend_sem, v_sem,
            device_id=(lax.rem(r + dr, n_row), c), device_id_type=MESH)

    def w_copy(j, dr):
        return pltpu.make_async_remote_copy(
            gout.at[j, 1], wc_out.at[j, lax.rem(r, halves)], gsend_sem, w_sem,
            device_id=(lax.rem(r + dr, n_row), c), device_id_type=MESH)

    def k_copy(dr):
        return pltpu.make_async_remote_copy(
            kmsg, krecv.at[r], ksend_sem, k_sem,
            device_id=(lax.rem(r + dr, n_row), c), device_id_type=MESH)

    gives_w = r // halves == c

    def spread(i):
        row = b0_ref[:, pl.ds(pl.multiple_of(i * LANES, LANES), LANES)]
        return jnp.broadcast_to(row, (LANES, LANES)).T

    def step(j, carry):
        m2 = pos > j + 1
        c0 = c0_ref[...]
        b0 = jnp.where(m2, c0, 0.0)
        b0_ref[...] = b0
        u_prev = u_ref[...]
        p_prev = p_ref[...]

        b_loc = b0[:, :rows]
        dvw = jnp.sum(vw[:, :rows] * b_loc, axis=1, keepdims=True)
        dpn = jnp.sum(panel[:, :rows] * b_loc, axis=1, keepdims=True)
        n0 = jnp.sum(b_loc * b_loc, axis=1, keepdims=True)
        kp = jnp.sum(u_prev[:, :rows] * p_prev[:, :rows], axis=1, keepdims=True)
        s32 = lax.broadcasted_iota(jnp.int32, (2 * K, LANES), 0)
        t32 = lax.broadcasted_iota(jnp.int32, (2 * K, LANES), 1)
        s24 = lax.broadcasted_iota(jnp.int32, (HEAD, LANES), 0)
        t24 = lax.broadcasted_iota(jnp.int32, (HEAD, LANES), 1)
        sc = jnp.sum(jnp.where(s32 == t32, dvw, 0.0), axis=0, keepdims=True)
        sc += jnp.sum(jnp.where(s24 + 2 * K == t24, dpn, 0.0), axis=0, keepdims=True)
        sc += jnp.where(l128 == 2 * K + HEAD, n0, 0.0) + jnp.where(l128 == 2 * K + HEAD + 1, kp, 0.0)

        def block(i, state):
            bc, accs = state
            pl.when(j == 0)(lambda: chunk(i).wait())
            nxt = spread(jnp.minimum(i + 1, blocks - 1))
            b3 = bc.reshape(LANES // 8, 8, LANES)
            part = pl.ds(pl.multiple_of(i * LANES, LANES), LANES)
            new = []
            for t in range(ctiles):
                x = tile[part, t * LANES:(t + 1) * LANES].reshape(LANES // 8, 8, LANES)
                new.append(accs[t] + jnp.sum(x * b3, axis=0))
            return nxt, tuple(new)

        zero = jnp.zeros((8, LANES), jnp.float32)
        _, accs = lax.fori_loop(0, blocks, block, (spread(0), (zero,) * ctiles))
        per = rows // LANES
        for h in range(halves):
            for t in range(per):
                msg[j, h, :, t * LANES:(t + 1) * LANES] = jnp.sum(accs[h * per + t], axis=0, keepdims=True)
            msg[j, h, :, rows:width] = sc

        each_target(lambda h, dc: send_copy(j, h, dc, False).start(), lambda h, dc: send_copy(j, h, dc, True).start())
        pltpu.make_async_copy(recv.at[j], recv.at[j], recv_sem.at[j]).wait()

        tot = jnp.sum(recv[j], axis=0)
        sc = tot[:, rows:width]
        wide = jnp.broadcast_to(sc, (2 * K, LANES))
        dots = jnp.sum(jnp.where(s32 == t32, wide, 0.0), axis=1, keepdims=True)
        n0 = sc[:, 2 * K + HEAD:2 * K + HEAD + 1]
        kp = sc[:, 2 * K + HEAD + 1:2 * K + HEAD + 2]
        tau_prev = s_ref[0:1, 0:1]
        bb_prev = s_ref[1:2, 0:1]
        kap = 0.5 * tau_prev * kp
        kap_out[pl.ds(j, 1), :] = jnp.broadcast_to(kap, (1, LANES))
        vw[pl.ds(K + j - 1, 1), :] = p_prev - kap * u_prev
        pj = panel[pl.ds(j, 1), :]
        pj1 = panel[pl.ds(j + 1, 1), :]
        col = c0 + 2.0 * kap * u_prev
        uj1 = lane_pick(u_prev[:, rows:width], l128, j + 1)
        aq = au_ref[...] - pj - uj1 * pj1
        yhead = jnp.where(l128 < HEAD, pltpu.roll(sc, LANES - 2 * K, 1), 0.0)
        y = jnp.concatenate([tot[:, :rows], yhead], axis=1) + 2.0 * kap * aq
        vb = dots[:K]
        wb = dots[K:]
        last = k16 == j - 1
        n1 = jnp.sum(jnp.where(last, vb, 0.0), axis=0, keepdims=True)
        b2 = jnp.maximum(n0 + 4.0 * kap * (n1 + kap * (bb_prev - uj1 * uj1)), 0.0)
        lead = lane_pick(col[:, rows:width], l128, j + 1)
        sig = jnp.sqrt(b2 + lead * lead)
        inv = 1.0 / (lead + sig)
        tau = 1.0 + lead / sig
        u = jnp.where(m2, col * inv, 0.0) + jnp.where(pos == j + 1, 1.0, 0.0)
        au = y * inv + pj1

        head = vw[:, rows:width]
        hj = lane_pick(head, l128, j)
        hj1 = lane_pick(head, l128, j + 1)
        uu = bb_prev + 1.0
        vup = jnp.where(last, uu, vu_ref[:, 0:1])
        wup = jnp.where(last, kp - kap * uu, wu_ref[:, 0:1])
        wb = jnp.where(last, wb - kap * vb, wb)
        vu = (vb + 2.0 * kap * (vup - hj[:K] - uj1 * hj1[:K])) * inv + hj1[:K]
        wu = (wb + 2.0 * kap * (wup - hj[K:] - uj1 * hj1[K:])) * inv + hj1[K:]
        v_all = vw[0:K, :]
        w_all = vw[K:2 * K, :]
        p = tau * (au - jnp.sum(v_all * wu + w_all * vu, axis=0, keepdims=True))
        pj1_entry = lane_pick(p[:, rows:width], l128, j + 1)
        c0n = pj1 - jnp.sum(v_all * hj1[K:] + w_all * hj1[:K], axis=0, keepdims=True) - pj1_entry * u - p
        gout[j, 0] = u[:, :rows]
        gout[j, 1] = p[:, :rows]
        c0_ref[...] = c0n
        u_ref[...] = u
        p_ref[...] = p
        au_ref[...] = au
        vu_ref[...] = jnp.broadcast_to(vu, (K, LANES))
        wu_ref[...] = jnp.broadcast_to(wu, (K, LANES))
        s_ref[0:1, :] = jnp.broadcast_to(tau, (1, LANES))
        s_ref[1:2, :] = jnp.broadcast_to(b2 * inv * inv, (1, LANES))
        coef_out[0:1, :] = jnp.where(l128 == j, tau, coef_out[0:1, :])
        coef_out[1:2, :] = jnp.where(l128 == j, -sig, coef_out[1:2, :])
        vw[pl.ds(j, 1), :] = u
        vw[pl.ds(K + j, 1), :] = p

        for dr in range(1, n_row):
            v_copy(j, dr).start()
        pltpu.make_async_copy(gout.at[j, 0], v_out.at[j, r], v_sem).start()

        @pl.when(gives_w)
        def _():
            for dr in range(1, n_row):
                w_copy(j, dr).start()
            pltpu.make_async_copy(gout.at[j, 1], wc_out.at[j, lax.rem(r, halves)], w_sem).start()
        return carry

    lax.fori_loop(0, K, step, 0)

    u = u_ref[...]
    p = p_ref[...]
    kp = jnp.sum(u[:, :rows] * p[:, :rows], axis=1, keepdims=True)
    kmsg[...] = jnp.broadcast_to(kp, (1, LANES))
    for dr in range(1, n_row):
        k_copy(dr).start()
    pltpu.make_async_copy(kmsg, krecv.at[r], k_sem).start()
    pltpu.make_async_copy(krecv, krecv, k_sem).wait()
    kap = 0.5 * s_ref[0:1, :] * jnp.sum(krecv[...], axis=0)
    kap_out[K:K + 1, :] = kap
    vw[2 * K - 1:2 * K, :] = p - kap[:, 0:1] * u
    vw_out[...] = vw[:, :rows]

    def drain(j, carry):
        each_target(lambda h, dc: send_copy(j, h, dc, False).wait_send(), None)
        for dr in range(1, n_row):
            v_copy(j, dr).wait_send()

        @pl.when(gives_w)
        def _():
            for dr in range(1, n_row):
                w_copy(j, dr).wait_send()
        return carry

    lax.fori_loop(0, K, drain, 0)

    @pl.when(c == 0)
    def _():
        @pl.when(r == 0)
        def _():
            for dr in range(n_row):
                for dc in range(n_col):
                    if dr or dc:
                        head_copy(dr, dc).wait_send()
        for dc in range(1, n_col):
            panel_copy(dc).wait_send()

    for dr in range(1, n_row):
        k_copy(dr).wait_send()
    pltpu.make_async_copy(v_out, v_out, v_sem).wait()
    pltpu.make_async_copy(wc_out, wc_out, w_sem).wait()


def pieces(x):
    hi = lax.reduce_precision(x, 8, 7)
    rest = x - hi
    mid = lax.reduce_precision(rest, 8, 7)
    low = lax.reduce_precision(rest - mid, 8, 7)
    return [part.astype(jnp.bfloat16) for part in (hi, mid, low)]


def make_per_device(n_row, n_col):
    def per_device(matrix):
        rows, cols = matrix.shape
        halves = cols // rows
        width = rows + LANES
        f32 = jnp.float32
        vmem = pl.BlockSpec(memory_space=pltpu.VMEM)
        anyspace = pl.BlockSpec(memory_space=pl.ANY)
        dma = pltpu.SemaphoreType.DMA

        def kernel(*refs):
            panel_kernel(rows, cols, n_row, n_col, *refs)

        v_full, wc, vw, coef, kap = pl.pallas_call(
            kernel,
            out_shape=(
                jax.ShapeDtypeStruct((K, n_row, 1, rows), f32),
                jax.ShapeDtypeStruct((K, halves, 1, rows), f32),
                jax.ShapeDtypeStruct((2 * K, rows), f32),
                jax.ShapeDtypeStruct((2, LANES), f32),
                jax.ShapeDtypeStruct((K + 1, LANES), f32),
            ),
            in_specs=[anyspace],
            out_specs=(anyspace, anyspace, vmem, vmem, vmem),
            scratch_shapes=[
                pltpu.VMEM((rows, cols), f32),
                pltpu.VMEM((rows, LANES), f32),
                pltpu.VMEM((HEAD, width), f32),
                pltpu.VMEM((2 * K, width), f32),
                pltpu.VMEM((K, halves, 1, width), f32),
                pltpu.VMEM((K, n_row, 1, width), f32),
                pltpu.VMEM((K, 2, 1, rows), f32),
                pltpu.VMEM((1, width), f32),
                pltpu.VMEM((1, width), f32),
                pltpu.VMEM((1, width), f32),
                pltpu.VMEM((1, width), f32),
                pltpu.VMEM((1, width), f32),
                pltpu.VMEM((K, LANES), f32),
                pltpu.VMEM((K, LANES), f32),
                pltpu.VMEM((8, LANES), f32),
                pltpu.VMEM((1, LANES), f32),
                pltpu.VMEM((n_row, 1, LANES), f32),
                dma((rows // LANES,)),
                dma, dma, dma, dma, dma,
                dma((K,)),
                dma, dma, dma, dma, dma,
            ],
            compiler_params=pltpu.CompilerParams(
                collective_id=0, has_side_effects=True, vmem_limit_bytes=48 * 1024 * 1024),
        )(matrix)
        reflectors = v_full.reshape(K, n_row * rows)
        c = lax.axis_index("col")
        v_cols = lax.dynamic_slice_in_dim(reflectors, c * cols, cols, 1)
        w_cols = wc.reshape(K, cols) - kap[1:, 0:1] * v_cols
        left = pieces(vw)
        right = pieces(jnp.concatenate([w_cols, v_cols], axis=0))
        order = ((0, 0), (0, 1), (1, 0), (1, 1), (0, 2), (2, 0))
        big_left = jnp.concatenate([left[a] for a, _ in order], axis=0)
        big_right = jnp.concatenate([right[b] for _, b in order], axis=0)
        change = lax.dot_general(big_left, big_right, (((0,), (0,)), ((), ())), preferred_element_type=f32)
        return matrix - change, reflectors, coef[:, :K]
    return per_device


def solution(mesh):
    return jax.shard_map(
        make_per_device(mesh.shape["row"], mesh.shape["col"]),
        mesh=mesh,
        in_specs=(P("row", "col"),),
        out_specs=(P("row", "col"), P(), P()),
        check_vma=False,
    )
```
